32 devices in a mesh: ctx: 8 (over y, x, core), head: 4 (over z).
Axes of the slice: x: 2, y: 2, z: 4, core: 2. Of those that a mesh axis runs over, the one named last changes fastest.
Arguments:
- head_inputs: bfloat16 [8192, 8192], P(('ctx', 'head')), may hold values from -6 to 6
- gate_inputs: bfloat16 [8192, 8192], P(('ctx', 'head')), may hold values from -6 to 6
- write_keys: bfloat16 [8192, 1024], P(('ctx', 'head')), may hold values from -6 to 6
- read_queries: bfloat16 [8192, 1024], P(('ctx', 'head')), may hold values from -0.5 to 0.5
- step_logits: bfloat16 [8192, 128], P(('ctx', 'head')), may hold values from -3 to 3
- step_bias: float32 [128], P('head'), may hold values from -6 to 0
- decay_log: float32 [128], P('head'), may hold values from -7 to -2
- skip_scale: float32 [128], P('head'), may hold values from 0.5 to 1.5
- norm_gain: float32 [8192], replicated, may hold values from 0.1 to 1.9
- document_starts: int32 [32], P('ctx'), may hold values from 0 to 256, as said below
Outputs:
- layer_output: bfloat16 [8192, 8192], P(('ctx', 'head'))
The draws below stay inside these ranges and needn't reach their ends.
Inputs may be any that keep to these rules, and one draw needn't show every extreme that they name: `document_starts`: each entry is the position within its block of 256 tokens at which a document starts, or 256 where none starts; the first block starts one at 0.
All inputs are finite; a program needn't handle non-finite values.
Results may differ from the reference program's by a relative error of at most 0.0058.
Values may be sent and summed in bfloat16 or wider, within the bound.
A program may use at most 128 MiB of HBM per device.

```python
import jax
import jax.numpy as jnp
from jax import lax

HEADS = 128
HEAD_DIM = 64
STATE = 128
GROUPS = 8
BLOCK = 256
INNER = 8192
TOKENS = 8192


def decay_heads(key):
    rand_key = jax.random.fold_in(key, 11)
    spread = jax.random.uniform(rand_key, (HEADS,), jnp.float32)
    memory = 30.0 * (TOKENS / 30.0) ** spread
    step_size = 2.0 / jnp.sqrt(memory)
    return (memory, step_size)


def draw_step_bias(key, part):
    memory, step_size = decay_heads(key)
    return jnp.log(jnp.expm1(step_size)).astype(jnp.float32)


def draw_decay_log(key, part):
    memory, step_size = decay_heads(key)
    return (-jnp.log(memory * step_size)).astype(jnp.float32)


def draw_document_starts(key, part):
    count = TOKENS // BLOCK
    spacing = max(count // 4, 2)
    raw_draw = jax.random.randint(jax.random.fold_in(key, 5), (count,), 0, spacing * BLOCK)
    starts = jnp.where(raw_draw < BLOCK, raw_draw, BLOCK)
    return starts.at[0].set(0).astype(jnp.int32)


def steps_of(key, extent, pieces, smallest, largest):
    factor_of, own = 1.0, jax.random.fold_in(key, 6)
    for dim, shards_of in pieces:
        draws = jnp.exp(jax.random.uniform(jax.random.fold_in(own, dim), (shards_of,), jnp.float32, smallest / len(pieces), largest / len(pieces)))
        factor_of = factor_of * jnp.repeat(draws, extent[dim] // shards_of).reshape([-1 if axis == dim else 1 for axis in range(len(extent))])
    return factor_of


def gaussian(key, extent, width, most, pieces=(), kind=jnp.bfloat16):
    drawn = width * jax.random.normal(key, extent, jnp.float32)
    if pieces:
        drawn = drawn * steps_of(key, extent, pieces, -0.22, 0.18)
    return jnp.clip(drawn, -most, most).astype(kind)


def setup_inputs(seed: int = 0) -> dict:
    seeds = jax.random.split(jax.random.key(seed), 11)
    return {
        "head_inputs": gaussian(seeds[0], (TOKENS, INNER), 1.0, 6.0, ((0, 32),)),
        "gate_inputs": gaussian(seeds[1], (TOKENS, INNER), 1.0, 6.0, ((0, 32),)),
        "write_keys": gaussian(seeds[2], (TOKENS, GROUPS * STATE), 1.0, 6.0, ((0, 32),)),
        "read_queries": gaussian(seeds[3], (TOKENS, GROUPS * STATE), STATE ** -0.5, 0.5, ((0, 32),)),
        "step_logits": gaussian(seeds[4], (TOKENS, HEADS), 0.5, 3.0, ((0, 32),)),
        "step_bias": draw_step_bias(jax.random.fold_in(seeds[10], 71), 0),
        "decay_log": draw_decay_log(jax.random.fold_in(seeds[10], 71), 0),
        "skip_scale": jnp.clip(0.5 + 1.0 * jax.random.uniform(seeds[7], (HEADS,), jnp.float32) ** steps_of(seeds[7], (HEADS,), ((0, 4),), -0.2, 0.2), 0.5, 1.5),
        "norm_gain": jnp.clip(1.0 + 0.18 * jax.random.normal(seeds[8], (INNER,), jnp.float32), 0.1, 1.9),
        "document_starts": draw_document_starts(jax.random.fold_in(seeds[10], 71), 0),
    }


def block_terms(block_x, block_b, block_c, block_logit, start_at, step_bias, decay_log):
    length = block_x.shape[0]
    per_group = block_x.shape[1] // block_b.shape[1]
    step_size = jax.nn.softplus(block_logit.astype(jnp.float32) + step_bias)
    log_decay = -jnp.exp(decay_log) * step_size
    cumulative = jnp.cumsum(log_decay, axis=0)
    position = jnp.arange(length, dtype=jnp.int32)
    segment = position >= start_at
    allowed = (segment[:, None] == segment[None, :]) & (position[:, None] >= position[None, :])
    scores = jnp.einsum('tgn,sgn->gts', block_c.astype(jnp.float32), block_b.astype(jnp.float32))
    scores = jnp.repeat(scores, per_group, axis=0)
    across = cumulative.T
    spread = across[:, :, None] - across[:, None, :]
    damping = jnp.where(allowed[None], jnp.exp(jnp.where(allowed[None], spread, 0.0)), 0.0)
    mixing = lax.optimization_barrier((damping * scores * step_size.T[:, None, :]).astype(jnp.bfloat16))
    inside = jnp.einsum('hts,shp->thp', mixing.astype(jnp.float32), block_x.astype(jnp.float32))
    keep = segment == segment[length - 1]
    tail = jnp.where(keep[:, None], jnp.exp(cumulative[length - 1][None, :] - cumulative), 0.0) * step_size
    scaled = lax.optimization_barrier((block_x.astype(jnp.float32) * tail[:, :, None]).astype(jnp.bfloat16))
    keys_heads = jnp.repeat(block_b, per_group, axis=1)
    written = jnp.einsum('thp,thn->hpn', scaled.astype(jnp.float32), keys_heads.astype(jnp.float32))
    carried = jnp.where(start_at >= length, jnp.exp(cumulative[length - 1]), 0.0)
    return (inside, written, carried, cumulative, segment)

def reference(head_inputs, gate_inputs, write_keys, read_queries, step_logits, step_bias, decay_log, skip_scale, norm_gain, document_starts):
    blocks = TOKENS // BLOCK
    per_group = HEADS // GROUPS
    x_blocks = head_inputs.reshape(blocks, BLOCK, HEADS, HEAD_DIM)
    b_blocks = write_keys.reshape(blocks, BLOCK, GROUPS, STATE)
    c_blocks = read_queries.reshape(blocks, BLOCK, GROUPS, STATE)
    logit_blocks = step_logits.reshape(blocks, BLOCK, HEADS)

    def advance(carry_state, items):
        block_x, block_b, block_c, block_logit, start_at = items
        inside, written, carried, cumulative, segment = block_terms(block_x, block_b, block_c, block_logit, start_at, step_bias, decay_log)
        frozen = lax.optimization_barrier(carry_state.astype(jnp.bfloat16))
        query_heads = jnp.repeat(block_c, per_group, axis=1)
        outside = jnp.einsum('thn,hpn->thp', query_heads.astype(jnp.float32), frozen.astype(jnp.float32))
        factor = jnp.where(segment[:, None], 0.0, jnp.exp(cumulative))
        mixed = (inside + outside * factor[:, :, None] + skip_scale[None, :, None] * block_x.astype(jnp.float32)).astype(jnp.bfloat16)
        next_state = carried[:, None, None] * carry_state + written
        return (next_state, mixed)
    initial = jnp.zeros((HEADS, HEAD_DIM, STATE), jnp.float32)
    _, mixed = lax.scan(advance, initial, (x_blocks, b_blocks, c_blocks, logit_blocks, document_starts))
    scanned = mixed.reshape(TOKENS, HEADS * HEAD_DIM)
    gated = scanned.astype(jnp.float32) * jax.nn.silu(gate_inputs.astype(jnp.float32))
    power = lax.optimization_barrier(jnp.mean(gated * gated, axis=-1, keepdims=True))
    return (gated * lax.rsqrt(power + 1e-05) * norm_gain).astype(jnp.bfloat16)
```

```python
import functools

import jax
import jax.numpy as jnp
from jax import lax
from jax.experimental import pallas as pl
from jax.experimental.pallas import tpu as pltpu
from jax.sharding import PartitionSpec as P

HEAD_DIM = 64
STATE = 128
BLOCK = 256
CHUNK = 512
SKEW = 2
MESH = pl.DeviceIdType.MESH
F32 = jnp.float32
BF16 = jnp.bfloat16


def split_terms(value, terms):
    parts = []
    for _ in range(terms):
        part = value.astype(BF16)
        parts.append(part)
        value = value - part.astype(F32)
    return parts


def spread_matrix(heads, first_head, width):
    row = lax.broadcasted_iota(jnp.int32, (2 * heads, width), 0)
    lane = lax.broadcasted_iota(jnp.int32, (2 * heads, width), 1)
    own = lane // HEAD_DIM + first_head
    return jnp.where((row == own) | (row == own + heads), 1.0, 0.0).astype(BF16)


def exchange_kernel(
    n, m, groups,
    x_ref, b_ref, logit_ref, param_ref, start_ref,
    frozen_ref, up_ref, down_ref, rows_ref,
    tail_ref, coef_ref, wide_ref, own_ref, sum_ref, before_ref,
    step_send, step_recv, fore_send, fore_recv, back_send, back_recv,
    param_in, decay_out, decay_in, hop_out, hop_in,
    param_sems, decay_sems, hop_sems, step_sems, fore_sems, back_sems,
):
    ci = lax.axis_index("ctx")
    zi = lax.axis_index("head")
    bits = m.bit_length() - 1
    length, inner = x_ref.shape
    heads = logit_ref.shape[1]
    count = inner // CHUNK
    per_group = count // groups

    def ctx_partner(j):
        bit = 1 << j
        upper = lax.rem(ci // bit, 2)
        return ci + bit - 2 * bit * upper, upper

    barrier = pltpu.get_barrier_semaphore()
    for d in range(1, n):
        pl.semaphore_signal(barrier, inc=1, device_id=(ci, lax.rem(zi + d, n)), device_id_type=MESH)
    for j in range(bits):
        pl.semaphore_signal(barrier, inc=1, device_id=(ctx_partner(j)[0], zi), device_id_type=MESH)
    pl.semaphore_wait(barrier, n - 1 + bits)

    def remote(src, dst, sems, index, device):
        return pltpu.make_async_remote_copy(
            src_ref=src, dst_ref=dst, send_sem=sems.at[(0, *index)], recv_sem=sems.at[(1, *index)],
            device_id=device, device_id_type=MESH,
        )

    def peer(d):
        return (ci, lax.rem(zi + d, n))

    param_copies = [
        remote(param_ref, param_in.at[d], param_sems, (d,), peer(d)) for d in range(1, n)
    ]
    for copy in param_copies:
        copy.start()
    for copy in param_copies:
        copy.wait()
    params = param_ref[...]
    for d in range(1, n):
        params = params + param_in[d]

    logits = logit_ref[...].astype(F32) + params[0:1]
    step = jnp.maximum(logits, 0.0) + jnp.log1p(jnp.exp(-jnp.abs(logits)))
    rate = -jnp.exp(params[1:2]) * step
    row = lax.broadcasted_iota(jnp.int32, (length, length), 0)
    col = lax.broadcasted_iota(jnp.int32, (length, length), 1)
    lower = jnp.where(row >= col, 1.0, 0.0).astype(BF16)
    cum = jnp.zeros((length, heads), F32)
    for part in split_terms(rate, 3)[::-1]:
        cum = cum + jnp.dot(lower, part, preferred_element_type=F32)
    last = cum[length - 1 : length]
    middle = cum[length // 2 - 1 : length // 2]
    start = start_ref[0:1, 0:1]
    position = lax.broadcasted_iota(jnp.int32, (length, heads), 0)
    begins = start < length
    keep = position >= jnp.where(begins, start, 0)
    tail = jnp.where(keep, jnp.exp(last - cum), 0.0) * step
    carried = jnp.where(begins, 0.0, jnp.exp(last))
    tail_ref[...] = jnp.concatenate(split_terms(tail, 2), axis=1)
    up_ref[...] = jnp.concatenate(split_terms(jnp.exp(cum - middle), 2), axis=1)
    down_ref[...] = jnp.concatenate(split_terms(jnp.exp(middle - cum) * step, 2), axis=1)

    decay_out[...] = jnp.broadcast_to(carried, decay_out.shape)
    decay_copies = [
        remote(decay_out, decay_in.at[d], decay_sems, (d,), peer(d)) for d in range(1, n)
    ]
    for copy in decay_copies:
        copy.start()
    for copy in decay_copies:
        copy.wait()
    before = jnp.ones((8, heads), F32)
    after = jnp.ones((8, heads), F32)
    for d in range(1, n):
        got = decay_in[d]
        before = before * jnp.where(zi >= d, got, 1.0)
        after = after * jnp.where(zi >= d, 1.0, got)
    own = jnp.broadcast_to(carried, (8, heads))
    total = before * own * after
    ahead = jnp.ones((8, heads), F32)
    coefs = [jnp.exp(jnp.broadcast_to(middle, (8, heads))), jnp.broadcast_to(params[2:3], (8, heads)), own, before, after]
    for j in range(bits):
        partner, upper = ctx_partner(j)
        hop_out[j] = total
        copy = remote(hop_out.at[j], hop_in.at[j], hop_sems, (j,), (partner, zi))
        copy.start()
        copy.wait()
        got = hop_in[j]
        is_upper = upper == 1
        coefs.append(jnp.where(is_upper, 1.0, got))
        coefs.append(jnp.where(is_upper, total, 1.0))
        coefs.append(jnp.where(is_upper, ahead, 0.0))
        ahead = jnp.where(is_upper, ahead * got, ahead)
        total = total * got
    slots = coef_ref.shape[0]
    pad = [jnp.zeros((1, heads), F32)] * (slots - len(coefs))
    table = jnp.concatenate([c[0:1] for c in coefs] + pad, axis=0)
    parts = split_terms(table, 3)
    first = jnp.concatenate(parts[:2], axis=1)

    def widen(k, _):
        matrix = spread_matrix(heads, k * (CHUNK // HEAD_DIM), CHUNK)
        wide = jnp.dot(first, matrix, preferred_element_type=F32)
        wide_ref[k] = wide
        rows_ref[k] = wide[0:8]
        return 0

    lax.fori_loop(0, count, widen, 0)

    fore_at = (bits + zi) * SKEW
    back_at = (bits + n - 1 - zi) * SKEW
    done_at = jnp.maximum(fore_at, back_at)

    def step_copy(j, k):
        return remote(step_send.at[j, k], step_recv.at[j, k], step_sems, (j, k), (ctx_partner(j)[0], zi))

    def fore_copy(k):
        return remote(fore_send.at[k], fore_recv.at[k], fore_sems, (k,), (ci, lax.rem(zi + 1, n)))

    def back_copy(k):
        return remote(back_send.at[k], back_recv.at[k], back_sems, (k,), (ci, lax.rem(zi + n - 1, n)))

    def line(k, slot):
        return wide_ref[k, slot : slot + 1, :]

    def iteration(t, _):
        @pl.when(t < count)
        def _():
            k = t
            matrix = spread_matrix(heads, k * (CHUNK // HEAD_DIM), CHUNK)
            weight = jnp.dot(tail_ref[...], matrix, preferred_element_type=F32)
            channels = pl.ds(pl.multiple_of(k * CHUNK, CHUNK), CHUNK)
            scaled = (x_ref[:, channels].astype(F32) * weight).astype(BF16)
            keys = b_ref[:, pl.ds(pl.multiple_of((k // per_group) * STATE, STATE), STATE)]
            written = lax.dot_general(keys, scaled, (((0,), (0,)), ((), ())), preferred_element_type=F32)
            own_ref[k] = written
            value = written * line(k, 4)
            sum_ref[k] = value
            before_ref[k] = jnp.zeros_like(value)
            step_send[0, k] = value.astype(BF16)
            step_copy(0, k).start()

        for j in range(bits):
            k = t - (j + 1) * SKEW

            @pl.when((k >= 0) & (k < count))
            def _(j=j, k=k):
                step_copy(j, k).wait_recv()
                got = step_recv[j, k].astype(F32)
                before_ref[k] += line(k, 7 + 3 * j) * got
                if j < bits - 1:
                    value = sum_ref[k] * line(k, 5 + 3 * j) + line(k, 6 + 3 * j) * got
                    sum_ref[k] = value
                    step_send[j + 1, k] = value.astype(BF16)
                    step_copy(j + 1, k).start()

        kf = t - fore_at

        @pl.when((kf >= 0) & (kf < count))
        def _():
            @pl.when(zi > 0)
            def _():
                fore_copy(kf).wait_recv()

            @pl.when(zi == 0)
            def _():
                fore_recv[kf] = jnp.zeros_like(fore_recv[kf])

            @pl.when(zi < n - 1)
            def _():
                arrived = fore_recv[kf].astype(F32) + line(kf, 3) * before_ref[kf]
                fore_send[kf] = (line(kf, 2) * arrived + own_ref[kf]).astype(BF16)
                fore_copy(kf).start()

        kb = t - back_at

        @pl.when((kb >= 0) & (kb < count))
        def _():
            @pl.when(zi < n - 1)
            def _():
                back_copy(kb).wait_recv()

            @pl.when(zi == n - 1)
            def _():
                back_recv[kb] = jnp.zeros_like(back_recv[kb])

            @pl.when(zi > 0)
            def _():
                back_send[kb] = (back_recv[kb].astype(F32) + before_ref[kb]).astype(BF16)
                back_copy(kb).start()

        kd = t - done_at

        @pl.when((kd >= 0) & (kd < count))
        def _():
            incoming = before_ref[kd] + back_recv[kd].astype(F32)
            frozen_ref[kd] = (fore_recv[kd].astype(F32) + line(kd, 3) * incoming).astype(BF16)

        return 0

    lax.fori_loop(0, count + (bits + n - 1) * SKEW, iteration, 0)

    def drain(k, _):
        for j in range(bits):
            step_copy(j, k).wait_send()

        @pl.when(zi < n - 1)
        def _():
            fore_copy(k).wait_send()

        @pl.when(zi > 0)
        def _():
            back_copy(k).wait_send()

        return 0

    lax.fori_loop(0, count, drain, 0)


def mix_kernel(
    x_ref, gate_ref, b_ref, c_ref, frozen_ref, up_ref, down_ref, rows_ref, start_ref, gain_ref,
    out_ref, gated_ref, power_ref,
):
    g = pl.program_id(0)
    length, width = x_ref.shape
    heads = up_ref.shape[1] // 2
    per_group = width // CHUNK
    start = start_ref[0:1, 0:1]
    row = lax.broadcasted_iota(jnp.int32, (length, length), 0)
    col = lax.broadcasted_iota(jnp.int32, (length, length), 1)
    allowed = (row >= col) & ((row >= start) == (col >= start))
    queries = c_ref[...]
    scores = lax.dot_general(queries, b_ref[...], (((1,), (1,)), ((), ())), preferred_element_type=F32)
    scores = jnp.where(allowed, scores, 0.0).astype(BF16)
    position = lax.broadcasted_iota(jnp.int32, (length, CHUNK), 0)
    power = jnp.zeros((length, 1), F32)
    for i in range(per_group):
        channels = slice(i * CHUNK, (i + 1) * CHUNK)
        k = g * per_group + i
        matrix = spread_matrix(heads, k * (CHUNK // HEAD_DIM), CHUNK)
        up = jnp.dot(up_ref[...], matrix, preferred_element_type=F32)
        down = jnp.dot(down_ref[...], matrix, preferred_element_type=F32)
        x = x_ref[:, channels].astype(F32)
        inside = jnp.dot(scores, (x * down).astype(BF16), preferred_element_type=F32)
        outside = jnp.dot(queries, frozen_ref[i], preferred_element_type=F32)
        outside = jnp.where(position < start, outside * rows_ref[i, 0:1, :], 0.0)
        mixed = (up * (inside + outside) + rows_ref[i, 1:2, :] * x).astype(BF16).astype(F32)
        gate = gate_ref[:, channels].astype(F32)
        gated = mixed * (gate / (1.0 + jnp.exp(-gate)))
        gated_ref[k] = gated
        power = power + jnp.sum(gated * gated, axis=1, keepdims=True)
    power_ref[...] = jnp.where(g == 0, 0.0, power_ref[...]) + jnp.broadcast_to(power, power_ref.shape)

    @pl.when(g == pl.num_programs(0) - 1)
    def _():
        count = gated_ref.shape[0]
        factor = lax.rsqrt(power_ref[:, 0:1] / (count * CHUNK) + 1e-05)
        for k in range(count):
            channels = slice(k * CHUNK, (k + 1) * CHUNK)
            out_ref[:, channels] = (gated_ref[k] * factor * gain_ref[0:1, channels]).astype(BF16)


def local(
    n, m,
    head_inputs, gate_inputs, write_keys, read_queries, step_logits,
    step_bias, decay_log, skip_scale, norm_gain, document_starts,
):
    length, inner = head_inputs.shape
    heads = step_logits.shape[1]
    groups = write_keys.shape[1] // STATE
    assert length <= BLOCK and BLOCK % length == 0 and m & (m - 1) == 0
    bits = m.bit_length() - 1
    count = inner // CHUNK
    per_group = count // groups
    zi = lax.axis_index("head")
    own = step_bias.shape[0]
    params = jnp.stack([step_bias, decay_log, skip_scale])
    params = lax.dynamic_update_slice(jnp.zeros((8, heads), F32), params, (0, zi * own))
    offset = lax.rem(zi * length, BLOCK)
    start = lax.dynamic_index_in_dim(document_starts, zi * length // BLOCK, keepdims=False) - offset
    start = jnp.where((start < 0) | (start >= length), length, start)
    start = jnp.broadcast_to(start, (8, 128)).astype(jnp.int32)

    slots = 24
    assert 5 + 3 * bits <= slots
    vmem = pl.BlockSpec(memory_space=pltpu.VMEM)
    piece = (count, STATE, CHUNK)
    dma = pltpu.SemaphoreType.DMA
    frozen, up, down, rows = pl.pallas_call(
        functools.partial(exchange_kernel, n, m, groups),
        out_shape=(
            jax.ShapeDtypeStruct(piece, BF16),
            jax.ShapeDtypeStruct((length, 2 * heads), BF16),
            jax.ShapeDtypeStruct((length, 2 * heads), BF16),
            jax.ShapeDtypeStruct((count, 8, CHUNK), F32),
        ),
        in_specs=[vmem] * 5,
        out_specs=(vmem,) * 4,
        scratch_shapes=[
            pltpu.VMEM((length, 2 * heads), BF16),
            pltpu.VMEM((24, heads), F32),
            pltpu.VMEM((count, 24, CHUNK), F32),
            pltpu.VMEM(piece, F32),
            pltpu.VMEM(piece, F32),
            pltpu.VMEM(piece, F32),
            pltpu.VMEM((bits, *piece), BF16),
            pltpu.VMEM((bits, *piece), BF16),
            pltpu.VMEM(piece, BF16),
            pltpu.VMEM(piece, BF16),
            pltpu.VMEM(piece, BF16),
            pltpu.VMEM(piece, BF16),
            pltpu.VMEM((n, 8, heads), F32),
            pltpu.VMEM((8, heads), F32),
            pltpu.VMEM((n, 8, heads), F32),
            pltpu.VMEM((bits, 8, heads), F32),
            pltpu.VMEM((bits, 8, heads), F32),
            dma((2, n)),
            dma((2, n)),
            dma((2, bits)),
            dma((2, bits, count)),
            dma((2, count)),
            dma((2, count)),
        ],
        compiler_params=pltpu.CompilerParams(
            collective_id=0, has_side_effects=True, vmem_limit_bytes=60 * 2**20
        ),
        name="exchange",
    )(head_inputs, write_keys, step_logits, params, start)

    width = per_group * CHUNK
    whole = lambda g: (0, 0)
    return pl.pallas_call(
        mix_kernel,
        grid=(groups,),
        out_shape=jax.ShapeDtypeStruct((length, inner), BF16),
        in_specs=[
            pl.BlockSpec((length, width), lambda g: (0, g)),
            pl.BlockSpec((length, width), lambda g: (0, g)),
            pl.BlockSpec((length, STATE), lambda g: (0, g)),
            pl.BlockSpec((length, STATE), lambda g: (0, g)),
            pl.BlockSpec((per_group, STATE, CHUNK), lambda g: (g, 0, 0)),
            pl.BlockSpec((length, 2 * heads), whole),
            pl.BlockSpec((length, 2 * heads), whole),
            pl.BlockSpec((per_group, 8, CHUNK), lambda g: (g, 0, 0)),
            pl.BlockSpec((8, 128), whole),
            pl.BlockSpec((1, inner), whole),
        ],
        out_specs=pl.BlockSpec((length, inner), whole),
        scratch_shapes=[
            pltpu.VMEM((count, length, CHUNK), F32),
            pltpu.VMEM((length, 128), F32),
        ],
        compiler_params=pltpu.CompilerParams(vmem_limit_bytes=60 * 2**20),
        name="mix",
    )(head_inputs, gate_inputs, write_keys, read_queries, frozen, up, down, rows, start, norm_gain[None])


def solution(mesh):
    tokens = P(("ctx", "head"), None)
    return jax.shard_map(
        functools.partial(local, mesh.shape["head"], mesh.shape["ctx"]),
        mesh=mesh,
        in_specs=(tokens,) * 5 + (P("head"), P("head"), P("head"), P(), P("ctx")),
        out_specs=tokens,
        check_vma=False,
    )
```

```python
import functools

import jax
import jax.numpy as jnp
from jax import lax
from jax.experimental import pallas as pl
from jax.experimental.pallas import tpu as pltpu
from jax.sharding import PartitionSpec as P

HEAD_DIM = 64
STATE = 128
BLOCK = 256
CHUNK = 256
SKEW = 2
ROWS = 32
MESH = pl.DeviceIdType.MESH
F32 = jnp.float32
BF16 = jnp.bfloat16


def split_terms(value, terms):
    parts = []
    for _ in range(terms):
        part = value.astype(BF16)
        parts.append(part)
        value = value - part.astype(F32)
    return parts


def spread_matrix(heads, first_head, width):
    row = lax.broadcasted_iota(jnp.int32, (2 * heads, width), 0)
    lane = lax.broadcasted_iota(jnp.int32, (2 * heads, width), 1)
    own = lane // HEAD_DIM + first_head
    return jnp.where((row == own) | (row == own + heads), 1.0, 0.0).astype(BF16)


def exchange_kernel(
    n, m, groups,
    x_hbm, b_ref, c_ref, logit_ref, bias_ref, decay_ref, skip_ref, starts_ref,
    mixed_hbm,
    x_ref, scores_ref, mixed_ref, param_ref,
    tail_ref, up_ref, down_ref, wide_ref, own_ref, sum_ref, before_ref,
    step_send, step_recv, fore_send, fore_recv, back_send, back_recv,
    param_in, decay_out, decay_in, hop_out, hop_in,
    param_sems, decay_sems, hop_sems, step_sems, fore_sems, back_sems, x_sem, mixed_sems,
):
    ci = lax.axis_index("ctx")
    zi = lax.axis_index("head")
    bits = m.bit_length() - 1
    length, inner = x_ref.shape
    heads = logit_ref.shape[1]
    count = inner // CHUNK
    per_group = count // groups
    chunk_heads = CHUNK // HEAD_DIM

    load_x = pltpu.make_async_copy(x_hbm, x_ref, x_sem)
    load_x.start()

    def ctx_partner(j):
        bit = 1 << j
        upper = lax.rem(ci // bit, 2)
        return ci + bit - 2 * bit * upper, upper

    barrier = pltpu.get_barrier_semaphore()
    for d in range(1, n):
        pl.semaphore_signal(barrier, inc=1, device_id=(ci, lax.rem(zi + d, n)), device_id_type=MESH)
    for j in range(bits):
        pl.semaphore_signal(barrier, inc=1, device_id=(ctx_partner(j)[0], zi), device_id_type=MESH)

    own_heads = bias_ref.shape[1]
    place = jnp.where(
        lax.broadcasted_iota(jnp.int32, (own_heads, heads), 0) + zi * own_heads
        == lax.broadcasted_iota(jnp.int32, (own_heads, heads), 1), 1.0, 0.0
    ).astype(BF16)
    raw = jnp.concatenate(
        [bias_ref[...], decay_ref[...], skip_ref[...], jnp.zeros((5, own_heads), F32)], axis=0
    )
    placed = jnp.zeros((8, heads), F32)
    for part in split_terms(raw, 3):
        placed = placed + jnp.dot(part, place, preferred_element_type=F32)
    param_ref[...] = placed
    pl.semaphore_wait(barrier, n - 1 + bits)

    def remote(src, dst, sems, index, device):
        return pltpu.make_async_remote_copy(
            src_ref=src, dst_ref=dst, send_sem=sems.at[(0, *index)], recv_sem=sems.at[(1, *index)],
            device_id=device, device_id_type=MESH,
        )

    def peer(d):
        return (ci, lax.rem(zi + d, n))

    param_copies = [
        remote(param_ref, param_in.at[d], param_sems, (d,), peer(d)) for d in range(1, n)
    ]
    for copy in param_copies:
        copy.start()

    offset = lax.rem(zi * length, BLOCK)
    starts = starts_ref[...].astype(F32)
    mine = lax.broadcasted_iota(jnp.int32, starts.shape, 1) == zi * length // BLOCK
    start = jnp.sum(jnp.where(mine, starts, 0.0), axis=1, keepdims=True) - offset.astype(F32)
    start = jnp.where((start < 0.0) | (start >= length), float(length), start)
    row = lax.broadcasted_iota(jnp.int32, (length, length), 0).astype(F32)
    col = lax.broadcasted_iota(jnp.int32, (length, length), 1).astype(F32)
    lower = jnp.where(row >= col, 1.0, 0.0)
    same = jnp.where(row >= start, 1.0, 0.0) == jnp.where(col >= start, 1.0, 0.0)
    allowed = jnp.where(same, lower, 0.0)
    for g in range(groups):
        part = slice(g * STATE, (g + 1) * STATE)
        scores = lax.dot_general(
            c_ref[:, part], b_ref[:, part], (((1,), (1,)), ((), ())), preferred_element_type=F32
        )
        scores_ref[g] = jnp.where(allowed > 0.0, scores, 0.0).astype(BF16)

    for copy in param_copies:
        copy.wait()
    params = param_ref[...]
    for d in range(1, n):
        params = params + param_in[d]

    logits = logit_ref[...].astype(F32) + params[0:1]
    step = jnp.maximum(logits, 0.0) + jnp.log1p(jnp.exp(-jnp.abs(logits)))
    rate = -jnp.exp(params[1:2]) * step
    lower = lower.astype(BF16)
    cum = jnp.zeros((length, heads), F32)
    for part in split_terms(rate, 3)[::-1]:
        cum = cum + jnp.dot(lower, part, preferred_element_type=F32)
    last = cum[length - 1 : length]
    middle = cum[length // 2 - 1 : length // 2]
    position = lax.broadcasted_iota(jnp.int32, (length, heads), 0).astype(F32)
    begins = start < length
    carried = jnp.where(begins, 0.0, jnp.exp(last))

    decay_out[...] = jnp.broadcast_to(carried, decay_out.shape)
    decay_copies = [
        remote(decay_out, decay_in.at[d], decay_sems, (d,), peer(d)) for d in range(1, n)
    ]
    for copy in decay_copies:
        copy.start()
    keep = position >= jnp.where(begins, start, 0.0)
    tail = jnp.where(keep, jnp.exp(last - cum), 0.0) * step
    tail_ref[...] = jnp.concatenate(split_terms(tail, 2), axis=1)
    up_ref[...] = jnp.concatenate(split_terms(jnp.exp(cum - middle), 2), axis=1)
    down_ref[...] = jnp.concatenate(split_terms(jnp.exp(middle - cum) * step, 2), axis=1)
    load_x.wait()
    for copy in decay_copies:
        copy.wait()
    before = jnp.ones((8, heads), F32)
    after = jnp.ones((8, heads), F32)
    for d in range(1, n):
        got = decay_in[d]
        before = before * jnp.where(zi >= d, got, 1.0)
        after = after * jnp.where(zi >= d, 1.0, got)
    own = jnp.broadcast_to(carried, (8, heads))
    total = before * own * after
    ahead = jnp.ones((8, heads), F32)
    after_parts = jnp.concatenate(split_terms(after, 2), axis=1)

    def step_copy(j, k):
        return remote(step_send.at[j, k], step_recv.at[j, k], step_sems, (j, k), (ctx_partner(j)[0], zi))

    def fore_copy(k):
        return remote(fore_send.at[k], fore_recv.at[k], fore_sems, (k,), (ci, lax.rem(zi + 1, n)))

    def back_copy(k):
        return remote(back_send.at[k], back_recv.at[k], back_sems, (k,), (ci, lax.rem(zi + n - 1, n)))

    def store_copy(k):
        channels = pl.ds(pl.multiple_of(k * CHUNK, CHUNK), CHUNK)
        return pltpu.make_async_copy(mixed_ref.at[k], mixed_hbm.at[:, channels], mixed_sems.at[k])

    def line(k, slot):
        return wide_ref[k, slot : slot + 1, :]

    is_last_upper = ctx_partner(bits - 1)[1] == 1
    is_last_lower = ctx_partner(bits - 1)[1] == 0

    def write(k, _):
        matrix = spread_matrix(heads, k * chunk_heads, CHUNK)
        weight = jnp.dot(tail_ref[...], matrix, preferred_element_type=F32)
        scale = jnp.dot(after_parts, matrix, preferred_element_type=F32)[0:1]
        channels = pl.ds(pl.multiple_of(k * CHUNK, CHUNK), CHUNK)
        scaled = (x_ref[:, channels].astype(F32) * weight).astype(BF16)
        keys = b_ref[:, pl.ds(pl.multiple_of((k // per_group) * STATE, STATE), STATE)]
        written = lax.dot_general(keys, scaled, (((0,), (0,)), ((), ())), preferred_element_type=F32)
        own_ref[k] = written
        value = written * scale
        sum_ref[k] = value
        step_send[0, k] = value.astype(BF16)
        step_copy(0, k).start()
        return 0

    middle_factor = jnp.broadcast_to(jnp.exp(middle), (8, heads))
    coefs = [middle_factor, jnp.broadcast_to(params[2:3], (8, heads)), own, before]
    for j in range(bits + 1):
        if j < bits:
            partner, upper = ctx_partner(j)
            hop_out[j] = total
            copy = remote(hop_out.at[j], hop_in.at[j], hop_sems, (j,), (partner, zi))
            copy.start()
        lax.fori_loop(j * count // (bits + 1), (j + 1) * count // (bits + 1), write, 0)
        if j < bits:
            copy.wait()
            got = hop_in[j]
            is_upper = upper == 1
            coefs.append(jnp.where(is_upper, 1.0, got))
            coefs.append(jnp.where(is_upper, total, 1.0))
            coefs.append(jnp.where(is_upper, ahead, 0.0))
            ahead = jnp.where(is_upper, ahead * got, ahead)
            total = total * got
    slots = wide_ref.shape[1]
    pad = [jnp.zeros((1, heads), F32)] * (slots - len(coefs))
    table = jnp.concatenate([c[0:1] for c in coefs] + pad, axis=0)
    table = jnp.concatenate(split_terms(table, 2), axis=1)

    fore_at = (bits - 1 + zi) * SKEW
    back_at = (bits - 1 + n - 1 - zi) * SKEW
    done_at = jnp.maximum(fore_at, back_at)

    def iteration(t, _):
        for j in range(bits):
            k = t - j * SKEW

            @pl.when((k >= 0) & (k < count))
            def _(j=j, k=k):
                if j == 0:
                    matrix = spread_matrix(heads, k * chunk_heads, CHUNK)
                    wide_ref[k] = jnp.dot(table, matrix, preferred_element_type=F32)
                    before_ref[k] = jnp.zeros_like(before_ref[k])

                def receive():
                    step_copy(j, k).wait_recv()
                    got = step_recv[j, k].astype(F32)
                    before_ref[k] += line(k, 6 + 3 * j) * got
                    return got

                if j == bits - 1:
                    @pl.when(is_last_upper)
                    def _():
                        receive()

                else:
                    got = receive()
                    value = sum_ref[k] * line(k, 4 + 3 * j) + line(k, 5 + 3 * j) * got
                    sum_ref[k] = value

                    def send():
                        step_send[j + 1, k] = value.astype(BF16)
                        step_copy(j + 1, k).start()

                    if j == bits - 2:
                        pl.when(is_last_lower)(send)
                    else:
                        send()

        kf = t - fore_at

        @pl.when((kf >= 0) & (kf < count))
        def _():
            @pl.when(zi > 0)
            def _():
                fore_copy(kf).wait_recv()

            @pl.when(zi == 0)
            def _():
                fore_recv[kf] = jnp.zeros_like(fore_recv[kf])

            @pl.when(zi < n - 1)
            def _():
                arrived = fore_recv[kf].astype(F32) + line(kf, 3) * before_ref[kf]
                fore_send[kf] = (line(kf, 2) * arrived + own_ref[kf]).astype(BF16)
                fore_copy(kf).start()

        kb = t - back_at

        @pl.when((kb >= 0) & (kb < count))
        def _():
            @pl.when(zi < n - 1)
            def _():
                back_copy(kb).wait_recv()

            @pl.when(zi == n - 1)
            def _():
                back_recv[kb] = jnp.zeros_like(back_recv[kb])

            @pl.when(zi > 0)
            def _():
                back_send[kb] = (back_recv[kb].astype(F32) + before_ref[kb]).astype(BF16)
                back_copy(kb).start()

        kd = t - done_at

        @pl.when((kd >= 0) & (kd < count))
        def _():
            incoming = before_ref[kd] + back_recv[kd].astype(F32)
            frozen = (fore_recv[kd].astype(F32) + line(kd, 3) * incoming).astype(BF16)
            matrix = spread_matrix(heads, kd * chunk_heads, CHUNK)
            up = jnp.dot(up_ref[...], matrix, preferred_element_type=F32)
            down = jnp.dot(down_ref[...], matrix, preferred_element_type=F32)
            x = x_ref[:, pl.ds(pl.multiple_of(kd * CHUNK, CHUNK), CHUNK)].astype(F32)
            group = kd // per_group
            inside = jnp.dot(scores_ref[group], (x * down).astype(BF16), preferred_element_type=F32)
            queries = c_ref[:, pl.ds(pl.multiple_of(group * STATE, STATE), STATE)]
            outside = jnp.dot(queries, frozen, preferred_element_type=F32)
            place_in = lax.broadcasted_iota(jnp.int32, outside.shape, 0).astype(F32)
            outside = jnp.where(place_in < start, outside * line(kd, 0), 0.0)
            mixed_ref[kd] = (up * (inside + outside) + line(kd, 1) * x).astype(BF16)
            store_copy(kd).start()

        return 0

    lax.fori_loop(0, count + (bits - 1 + n - 1) * SKEW, iteration, 0)

    def drain(k, _):
        for j in range(bits - 1):
            step_copy(j, k).wait_send()

        @pl.when(is_last_lower)
        def _():
            step_copy(bits - 1, k).wait_send()

        @pl.when(zi < n - 1)
        def _():
            fore_copy(k).wait_send()

        @pl.when(zi > 0)
        def _():
            back_copy(k).wait_send()

        store_copy(k).wait()
        return 0

    lax.fori_loop(0, count, drain, 0)


def norm_kernel(mixed_ref, gate_ref, gain_ref, out_ref, gated_ref):
    rows, inner = mixed_ref.shape
    width = 1024
    power = jnp.zeros((rows, 1), F32)
    for i in range(inner // width):
        channels = slice(i * width, (i + 1) * width)
        gate = gate_ref[:, channels].astype(F32)
        gated = mixed_ref[:, channels].astype(F32) * (gate / (1.0 + jnp.exp(-gate)))
        gated_ref[:, channels] = gated
        power = power + jnp.sum(gated * gated, axis=1, keepdims=True)
    factor = lax.rsqrt(power / inner + 1e-05)
    for i in range(inner // width):
        channels = slice(i * width, (i + 1) * width)
        out_ref[:, channels] = (gated_ref[:, channels] * factor * gain_ref[:, channels]).astype(BF16)


def local(
    n, m,
    head_inputs, gate_inputs, write_keys, read_queries, step_logits,
    step_bias, decay_log, skip_scale, norm_gain, document_starts,
):
    length, inner = head_inputs.shape
    heads = step_logits.shape[1]
    groups = write_keys.shape[1] // STATE
    assert length <= BLOCK and BLOCK % length == 0 and m & (m - 1) == 0 and m > 1
    bits = m.bit_length() - 1
    count = inner // CHUNK

    slots = 24
    assert 4 + 3 * bits <= slots
    vmem = pl.BlockSpec(memory_space=pltpu.VMEM)
    hbm = pl.BlockSpec(memory_space=pl.ANY)
    piece = (count, STATE, CHUNK)
    dma = pltpu.SemaphoreType.DMA
    mixed = pl.pallas_call(
        functools.partial(exchange_kernel, n, m, groups),
        out_shape=jax.ShapeDtypeStruct((length, inner), BF16),
        in_specs=[hbm] + [vmem] * 7,
        out_specs=hbm,
        scratch_shapes=[
            pltpu.VMEM((length, inner), BF16),
            pltpu.VMEM((groups, length, length), BF16),
            pltpu.VMEM((count, length, CHUNK), BF16),
            pltpu.VMEM((8, heads), F32),
            pltpu.VMEM((length, 2 * heads), BF16),
            pltpu.VMEM((length, 2 * heads), BF16),
            pltpu.VMEM((length, 2 * heads), BF16),
            pltpu.VMEM((count, slots, CHUNK), F32),
            pltpu.VMEM(piece, F32),
            pltpu.VMEM(piece, F32),
            pltpu.VMEM(piece, F32),
            pltpu.VMEM((bits, *piece), BF16),
            pltpu.VMEM((bits, *piece), BF16),
            pltpu.VMEM(piece, BF16),
            pltpu.VMEM(piece, BF16),
            pltpu.VMEM(piece, BF16),
            pltpu.VMEM(piece, BF16),
            pltpu.VMEM((n, 8, heads), F32),
            pltpu.VMEM((8, heads), F32),
            pltpu.VMEM((n, 8, heads), F32),
            pltpu.VMEM((bits, 8, heads), F32),
            pltpu.VMEM((bits, 8, heads), F32),
            dma((2, n)),
            dma((2, n)),
            dma((2, bits)),
            dma((2, bits, count)),
            dma((2, count)),
            dma((2, count)),
            dma,
            dma((count,)),
        ],
        compiler_params=pltpu.CompilerParams(
            collective_id=0, has_side_effects=True, vmem_limit_bytes=60 * 2**20
        ),
        name="exchange",
    )(
        head_inputs, write_keys, read_queries, step_logits,
        step_bias[None], decay_log[None], skip_scale[None], document_starts[None],
    )

    tile = min(length, ROWS)
    tokens = pl.BlockSpec((tile, inner), lambda i: (i, 0))
    return pl.pallas_call(
        norm_kernel,
        grid=(length // tile,),
        out_shape=jax.ShapeDtypeStruct((length, inner), BF16),
        in_specs=[tokens, tokens, pl.BlockSpec((1, inner), lambda i: (0, 0))],
        out_specs=tokens,
        scratch_shapes=[pltpu.VMEM((tile, inner), F32)],
        compiler_params=pltpu.CompilerParams(vmem_limit_bytes=32 * 2**20),
        name="norm",
    )(mixed, gate_inputs, norm_gain[None])


def solution(mesh):
    tokens = P(("ctx", "head"), None)
    return jax.shard_map(
        functools.partial(local, mesh.shape["head"], mesh.shape["ctx"]),
        mesh=mesh,
        in_specs=(tokens,) * 5 + (P("head"), P("head"), P("head"), P(), P("ctx")),
        out_specs=tokens,
        check_vma=False,
    )
```

```python
import functools

import jax
import jax.numpy as jnp
from jax import lax
from jax.experimental import pallas as pl
from jax.experimental.pallas import tpu as pltpu
from jax.sharding import PartitionSpec as P

HEAD_DIM = 64
STATE = 128
BLOCK = 256
CHUNK = 256
SKEW = 3
EARLY = 2
ROWS = 32
MESH = pl.DeviceIdType.MESH
F32 = jnp.float32
BF16 = jnp.bfloat16


def split_terms(value, terms):
    parts = []
    for _ in range(terms):
        part = value.astype(BF16)
        parts.append(part)
        value = value - part.astype(F32)
    return parts


def spread_matrix(heads, first_head, width):
    row = lax.broadcasted_iota(jnp.int32, (2 * heads, width), 0)
    lane = lax.broadcasted_iota(jnp.int32, (2 * heads, width), 1)
    own = lane // HEAD_DIM + first_head
    return jnp.where((row == own) | (row == own + heads), 1.0, 0.0).astype(BF16)


def exchange_kernel(
    n, m, groups,
    x_hbm, b_ref, c_ref, logit_ref, bias_ref, decay_ref, skip_ref, starts_ref,
    mixed_hbm,
    x_ref, scores_ref, mixed_ref, param_ref,
    tail_ref, up_ref, down_ref, wide_ref, own_ref, sum_ref, before_ref,
    step_send, step_recv, fore_send, fore_recv, back_send, back_recv,
    param_in, decay_out, decay_in, hop_out, hop_in,
    param_sems, decay_sems, hop_sems, step_sems, fore_sems, back_sems, x_sem, mixed_sems,
):
    ci = lax.axis_index("ctx")
    zi = lax.axis_index("head")
    bits = m.bit_length() - 1
    length, inner = x_ref.shape
    heads = logit_ref.shape[1]
    count = inner // CHUNK
    per_group = count // groups
    chunk_heads = CHUNK // HEAD_DIM

    load_x = pltpu.make_async_copy(x_hbm, x_ref, x_sem)
    load_x.start()

    def ctx_partner(j):
        bit = 1 << j
        upper = lax.rem(ci // bit, 2)
        return ci + bit - 2 * bit * upper, upper

    barrier = pltpu.get_barrier_semaphore()
    for d in range(1, n):
        pl.semaphore_signal(barrier, inc=1, device_id=(ci, lax.rem(zi + d, n)), device_id_type=MESH)
    for j in range(bits):
        pl.semaphore_signal(barrier, inc=1, device_id=(ctx_partner(j)[0], zi), device_id_type=MESH)

    own_heads = bias_ref.shape[1]
    place = jnp.where(
        lax.broadcasted_iota(jnp.int32, (own_heads, heads), 0) + zi * own_heads
        == lax.broadcasted_iota(jnp.int32, (own_heads, heads), 1), 1.0, 0.0
    ).astype(BF16)
    raw = jnp.concatenate(
        [bias_ref[...], decay_ref[...], skip_ref[...], jnp.zeros((5, own_heads), F32)], axis=0
    )
    placed = jnp.zeros((8, heads), F32)
    for part in split_terms(raw, 3):
        placed = placed + jnp.dot(part, place, preferred_element_type=F32)
    param_ref[...] = placed
    pl.semaphore_wait(barrier, n - 1 + bits)

    def remote(src, dst, sems, index, device):
        return pltpu.make_async_remote_copy(
            src_ref=src, dst_ref=dst, send_sem=sems.at[(0, *index)], recv_sem=sems.at[(1, *index)],
            device_id=device, device_id_type=MESH,
        )

    def peer(d):
        return (ci, lax.rem(zi + d, n))

    param_copies = [
        remote(param_ref, param_in.at[d], param_sems, (d,), peer(d)) for d in range(1, n)
    ]
    for copy in param_copies:
        copy.start()

    offset = lax.rem(zi * length, BLOCK)
    starts = starts_ref[...].astype(F32)
    mine = lax.broadcasted_iota(jnp.int32, starts.shape, 1) == zi * length // BLOCK
    start = jnp.sum(jnp.where(mine, starts, 0.0), axis=1, keepdims=True) - offset.astype(F32)
    start = jnp.where((start < 0.0) | (start >= length), float(length), start)
    row = lax.broadcasted_iota(jnp.int32, (length, length), 0).astype(F32)
    col = lax.broadcasted_iota(jnp.int32, (length, length), 1).astype(F32)
    lower = jnp.where(row >= col, 1.0, 0.0)
    same = jnp.where(row >= start, 1.0, 0.0) == jnp.where(col >= start, 1.0, 0.0)
    allowed = jnp.where(same, lower, 0.0)
    for g in range(groups):
        part = slice(g * STATE, (g + 1) * STATE)
        scores = lax.dot_general(
            c_ref[:, part], b_ref[:, part], (((1,), (1,)), ((), ())), preferred_element_type=F32
        )
        scores_ref[g] = jnp.where(allowed > 0.0, scores, 0.0).astype(BF16)

    for copy in param_copies:
        copy.wait()
    params = param_ref[...]
    for d in range(1, n):
        params = params + param_in[d]

    logits = logit_ref[...].astype(F32) + params[0:1]
    step = jnp.maximum(logits, 0.0) + jnp.log1p(jnp.exp(-jnp.abs(logits)))
    rate = -jnp.exp(params[1:2]) * step
    lower = lower.astype(BF16)
    cum = jnp.zeros((length, heads), F32)
    for part in split_terms(rate, 3)[::-1]:
        cum = cum + jnp.dot(lower, part, preferred_element_type=F32)
    last = cum[length - 1 : length]
    middle = cum[length // 2 - 1 : length // 2]
    position = lax.broadcasted_iota(jnp.int32, (length, heads), 0).astype(F32)
    begins = start < length
    carried = jnp.where(begins, 0.0, jnp.exp(last))

    decay_out[...] = jnp.broadcast_to(carried, decay_out.shape)
    decay_copies = [
        remote(decay_out, decay_in.at[d], decay_sems, (d,), peer(d)) for d in range(1, n)
    ]
    for copy in decay_copies:
        copy.start()
    keep = position >= jnp.where(begins, start, 0.0)
    tail = jnp.where(keep, jnp.exp(last - cum), 0.0) * step
    tail_ref[...] = jnp.concatenate(split_terms(tail, 2), axis=1)
    up_ref[...] = jnp.concatenate(split_terms(jnp.exp(cum - middle), 2), axis=1)
    down_ref[...] = jnp.concatenate(split_terms(jnp.exp(middle - cum) * step, 2), axis=1)
    load_x.wait()
    for copy in decay_copies:
        copy.wait()
    before = jnp.ones((8, heads), F32)
    after = jnp.ones((8, heads), F32)
    for d in range(1, n):
        got = decay_in[d]
        before = before * jnp.where(zi >= d, got, 1.0)
        after = after * jnp.where(zi >= d, 1.0, got)
    own = jnp.broadcast_to(carried, (8, heads))
    total = before * own * after
    ahead = jnp.ones((8, heads), F32)
    after_parts = jnp.concatenate(split_terms(after, 2), axis=1)

    def step_copy(j, k):
        return remote(step_send.at[j, k], step_recv.at[j, k], step_sems, (j, k), (ctx_partner(j)[0], zi))

    def fore_copy(k):
        return remote(fore_send.at[k], fore_recv.at[k], fore_sems, (k,), (ci, lax.rem(zi + 1, n)))

    def back_copy(k):
        return remote(back_send.at[k], back_recv.at[k], back_sems, (k,), (ci, lax.rem(zi + n - 1, n)))

    def store_copy(k):
        channels = pl.ds(pl.multiple_of(k * CHUNK, CHUNK), CHUNK)
        return pltpu.make_async_copy(mixed_ref.at[k], mixed_hbm.at[:, channels], mixed_sems.at[k])

    def line(k, slot):
        return wide_ref[k, slot : slot + 1, :]

    is_last_upper = ctx_partner(bits - 1)[1] == 1
    is_last_lower = ctx_partner(bits - 1)[1] == 0

    def write(k, _):
        matrix = spread_matrix(heads, k * chunk_heads, CHUNK)
        weight = jnp.dot(tail_ref[...], matrix, preferred_element_type=F32)
        scale = jnp.dot(after_parts, matrix, preferred_element_type=F32)[0:1]
        channels = pl.ds(pl.multiple_of(k * CHUNK, CHUNK), CHUNK)
        scaled = (x_ref[:, channels].astype(F32) * weight).astype(BF16)
        keys = b_ref[:, pl.ds(pl.multiple_of((k // per_group) * STATE, STATE), STATE)]
        written = lax.dot_general(keys, scaled, (((0,), (0,)), ((), ())), preferred_element_type=F32)
        own_ref[k] = written
        value = written * scale
        sum_ref[k] = value
        step_send[0, k] = value.astype(BF16)
        step_copy(0, k).start()
        return 0

    middle_factor = jnp.broadcast_to(jnp.exp(middle), (8, heads))
    coefs = [middle_factor, jnp.broadcast_to(params[2:3], (8, heads)), own, before]
    for j in range(bits):
        partner, upper = ctx_partner(j)
        hop_out[j] = total
        copy = remote(hop_out.at[j], hop_in.at[j], hop_sems, (j,), (partner, zi))
        copy.start()
        lax.fori_loop(j * EARLY, (j + 1) * EARLY, write, 0)
        copy.wait()
        got = hop_in[j]
        is_upper = upper == 1
        coefs.append(jnp.where(is_upper, 1.0, got))
        coefs.append(jnp.where(is_upper, total, 1.0))
        coefs.append(jnp.where(is_upper, ahead, 0.0))
        ahead = jnp.where(is_upper, ahead * got, ahead)
        total = total * got
    slots = wide_ref.shape[1]
    pad = [jnp.zeros((1, heads), F32)] * (slots - len(coefs))
    table = jnp.concatenate([c[0:1] for c in coefs] + pad, axis=0)
    table = jnp.concatenate(split_terms(table, 2), axis=1)

    fore_at = (bits - 1 + zi) * SKEW
    back_at = (bits - 1 + n - 1 - zi) * SKEW
    done_at = jnp.maximum(fore_at, back_at)

    def iteration(t, _):
        kw = t + bits * EARLY

        @pl.when(kw < count)
        def _():
            write(kw, 0)

        for j in range(bits):
            k = t - j * SKEW

            @pl.when((k >= 0) & (k < count))
            def _(j=j, k=k):
                if j == 0:
                    matrix = spread_matrix(heads, k * chunk_heads, CHUNK)
                    wide_ref[k] = jnp.dot(table, matrix, preferred_element_type=F32)
                    before_ref[k] = jnp.zeros_like(before_ref[k])

                def receive():
                    step_copy(j, k).wait_recv()
                    got = step_recv[j, k].astype(F32)
                    before_ref[k] += line(k, 6 + 3 * j) * got
                    return got

                if j == bits - 1:
                    @pl.when(is_last_upper)
                    def _():
                        receive()

                else:
                    got = receive()
                    value = sum_ref[k] * line(k, 4 + 3 * j) + line(k, 5 + 3 * j) * got
                    sum_ref[k] = value

                    def send():
                        step_send[j + 1, k] = value.astype(BF16)
                        step_copy(j + 1, k).start()

                    if j == bits - 2:
                        pl.when(is_last_lower)(send)
                    else:
                        send()

        kf = t - fore_at

        @pl.when((kf >= 0) & (kf < count))
        def _():
            @pl.when(zi > 0)
            def _():
                fore_copy(kf).wait_recv()

            @pl.when(zi == 0)
            def _():
                fore_recv[kf] = jnp.zeros_like(fore_recv[kf])

            @pl.when(zi < n - 1)
            def _():
                arrived = fore_recv[kf].astype(F32) + line(kf, 3) * before_ref[kf]
                fore_send[kf] = (line(kf, 2) * arrived + own_ref[kf]).astype(BF16)
                fore_copy(kf).start()

        kb = t - back_at

        @pl.when((kb >= 0) & (kb < count))
        def _():
            @pl.when(zi < n - 1)
            def _():
                back_copy(kb).wait_recv()

            @pl.when(zi == n - 1)
            def _():
                back_recv[kb] = jnp.zeros_like(back_recv[kb])

            @pl.when(zi > 0)
            def _():
                back_send[kb] = (back_recv[kb].astype(F32) + before_ref[kb]).astype(BF16)
                back_copy(kb).start()

        kd = t - done_at

        @pl.when((kd >= 0) & (kd < count))
        def _():
            incoming = before_ref[kd] + back_recv[kd].astype(F32)
            frozen = (fore_recv[kd].astype(F32) + line(kd, 3) * incoming).astype(BF16)
            matrix = spread_matrix(heads, kd * chunk_heads, CHUNK)
            up = jnp.dot(up_ref[...], matrix, preferred_element_type=F32)
            down = jnp.dot(down_ref[...], matrix, preferred_element_type=F32)
            x = x_ref[:, pl.ds(pl.multiple_of(kd * CHUNK, CHUNK), CHUNK)].astype(F32)
            group = kd // per_group
            inside = jnp.dot(scores_ref[group], (x * down).astype(BF16), preferred_element_type=F32)
            queries = c_ref[:, pl.ds(pl.multiple_of(group * STATE, STATE), STATE)]
            outside = jnp.dot(queries, frozen, preferred_element_type=F32)
            place_in = lax.broadcasted_iota(jnp.int32, outside.shape, 0).astype(F32)
            outside = jnp.where(place_in < start, outside * line(kd, 0), 0.0)
            mixed_ref[kd] = (up * (inside + outside) + line(kd, 1) * x).astype(BF16)
            store_copy(kd).start()

        return 0

    lax.fori_loop(0, count + (bits - 1 + n - 1) * SKEW, iteration, 0)

    def drain(k, _):
        for j in range(bits - 1):
            step_copy(j, k).wait_send()

        @pl.when(is_last_lower)
        def _():
            step_copy(bits - 1, k).wait_send()

        @pl.when(zi < n - 1)
        def _():
            fore_copy(k).wait_send()

        @pl.when(zi > 0)
        def _():
            back_copy(k).wait_send()

        store_copy(k).wait()
        return 0

    lax.fori_loop(0, count, drain, 0)


def norm_kernel(mixed_ref, gate_ref, gain_ref, out_ref, gated_ref):
    rows, inner = mixed_ref.shape
    width = 1024
    power = jnp.zeros((rows, 1), F32)
    for i in range(inner // width):
        channels = slice(i * width, (i + 1) * width)
        gate = gate_ref[:, channels].astype(F32)
        gated = mixed_ref[:, channels].astype(F32) * (gate / (1.0 + jnp.exp(-gate)))
        gated_ref[:, channels] = gated
        power = power + jnp.sum(gated * gated, axis=1, keepdims=True)
    factor = lax.rsqrt(power / inner + 1e-05)
    for i in range(inner // width):
        channels = slice(i * width, (i + 1) * width)
        out_ref[:, channels] = (gated_ref[:, channels] * factor * gain_ref[:, channels]).astype(BF16)


def local(
    n, m,
    head_inputs, gate_inputs, write_keys, read_queries, step_logits,
    step_bias, decay_log, skip_scale, norm_gain, document_starts,
):
    length, inner = head_inputs.shape
    heads = step_logits.shape[1]
    groups = write_keys.shape[1] // STATE
    assert length <= BLOCK and BLOCK % length == 0 and m & (m - 1) == 0 and m > 1
    bits = m.bit_length() - 1
    count = inner // CHUNK

    slots = 24
    assert bits * EARLY <= count and 4 + 3 * bits <= slots
    vmem = pl.BlockSpec(memory_space=pltpu.VMEM)
    hbm = pl.BlockSpec(memory_space=pl.ANY)
    piece = (count, STATE, CHUNK)
    dma = pltpu.SemaphoreType.DMA
    mixed = pl.pallas_call(
        functools.partial(exchange_kernel, n, m, groups),
        out_shape=jax.ShapeDtypeStruct((length, inner), BF16),
        in_specs=[hbm] + [vmem] * 7,
        out_specs=hbm,
        scratch_shapes=[
            pltpu.VMEM((length, inner), BF16),
            pltpu.VMEM((groups, length, length), BF16),
            pltpu.VMEM((count, length, CHUNK), BF16),
            pltpu.VMEM((8, heads), F32),
            pltpu.VMEM((length, 2 * heads), BF16),
            pltpu.VMEM((length, 2 * heads), BF16),
            pltpu.VMEM((length, 2 * heads), BF16),
            pltpu.VMEM((count, slots, CHUNK), F32),
            pltpu.VMEM(piece, F32),
            pltpu.VMEM(piece, F32),
            pltpu.VMEM(piece, F32),
            pltpu.VMEM((bits, *piece), BF16),
            pltpu.VMEM((bits, *piece), BF16),
            pltpu.VMEM(piece, BF16),
            pltpu.VMEM(piece, BF16),
            pltpu.VMEM(piece, BF16),
            pltpu.VMEM(piece, BF16),
            pltpu.VMEM((n, 8, heads), F32),
            pltpu.VMEM((8, heads), F32),
            pltpu.VMEM((n, 8, heads), F32),
            pltpu.VMEM((bits, 8, heads), F32),
            pltpu.VMEM((bits, 8, heads), F32),
            dma((2, n)),
            dma((2, n)),
            dma((2, bits)),
            dma((2, bits, count)),
            dma((2, count)),
            dma((2, count)),
            dma,
            dma((count,)),
        ],
        compiler_params=pltpu.CompilerParams(
            collective_id=0, has_side_effects=True, vmem_limit_bytes=48 * 2**20
        ),
        name="exchange",
    )(
        head_inputs, write_keys, read_queries, step_logits,
        step_bias[None], decay_log[None], skip_scale[None], document_starts[None],
    )

    tile = min(length, ROWS)
    tokens = pl.BlockSpec((tile, inner), lambda i: (i, 0))
    return pl.pallas_call(
        norm_kernel,
        grid=(length // tile,),
        out_shape=jax.ShapeDtypeStruct((length, inner), BF16),
        in_specs=[tokens, tokens, pl.BlockSpec((1, inner), lambda i: (0, 0))],
        out_specs=tokens,
        scratch_shapes=[pltpu.VMEM((tile, inner), F32)],
        compiler_params=pltpu.CompilerParams(vmem_limit_bytes=20 * 2**20),
        name="norm",
    )(mixed, gate_inputs, norm_gain[None])


def solution(mesh):
    tokens = P(("ctx", "head"), None)
    return jax.shard_map(
        functools.partial(local, mesh.shape["head"], mesh.shape["ctx"]),
        mesh=mesh,
        in_specs=(tokens,) * 5 + (P("head"), P("head"), P("head"), P(), P("ctx")),
        out_specs=tokens,
        check_vma=False,
    )
```

```python
import functools

import jax
import jax.numpy as jnp
from jax import lax
from jax.experimental import pallas as pl
from jax.experimental.pallas import tpu as pltpu
from jax.sharding import PartitionSpec as P

HEAD_DIM = 64
STATE = 128
BLOCK = 256
CHUNK = 256
SKEW = 3
EARLY = 2
ROWS = 32
MESH = pl.DeviceIdType.MESH
F32 = jnp.float32
BF16 = jnp.bfloat16


def split_terms(value, terms):
    parts = []
    for _ in range(terms):
        part = value.astype(BF16)
        parts.append(part)
        value = value - part.astype(F32)
    return parts


def spread_matrix(heads, first_head, width):
    row = lax.broadcasted_iota(jnp.int32, (2 * heads, width), 0)
    lane = lax.broadcasted_iota(jnp.int32, (2 * heads, width), 1)
    own = lane // HEAD_DIM + first_head
    return jnp.where((row == own) | (row == own + heads), 1.0, 0.0).astype(BF16)


def exchange_kernel(
    n, m, groups,
    x_hbm, b_hbm, c_hbm, logit_hbm, bias_hbm, decay_hbm, skip_hbm, starts_hbm,
    mixed_hbm,
    x_ref, b_ref, c_ref, logit_ref, bias_ref, decay_ref, skip_ref, starts_ref, scores_ref, mixed_ref, param_ref,
    tail_ref, up_ref, down_ref, wide_ref, own_ref, sum_ref, before_ref,
    step_send, step_recv, fore_send, fore_recv, back_send, back_recv,
    param_in, decay_out, decay_in, hop_out, hop_in,
    param_sems, decay_sems, hop_sems, step_sems, fore_sems, back_sems, load_sems, mixed_sems,
):
    ci = lax.axis_index("ctx")
    zi = lax.axis_index("head")
    bits = m.bit_length() - 1
    length, inner = x_ref.shape
    heads = logit_ref.shape[1]
    count = inner // CHUNK
    per_group = count // groups
    chunk_heads = CHUNK // HEAD_DIM

    pairs = (
        (bias_hbm, bias_ref), (decay_hbm, decay_ref), (skip_hbm, skip_ref), (starts_hbm, starts_ref),
        (b_hbm, b_ref), (c_hbm, c_ref), (logit_hbm, logit_ref), (x_hbm, x_ref),
    )
    loads = [pltpu.make_async_copy(src, dst, load_sems.at[i]) for i, (src, dst) in enumerate(pairs)]
    for load in loads:
        load.start()

    def ctx_partner(j):
        bit = 1 << j
        upper = lax.rem(ci // bit, 2)
        return ci + bit - 2 * bit * upper, upper

    barrier = pltpu.get_barrier_semaphore()
    for d in range(1, n):
        pl.semaphore_signal(barrier, inc=1, device_id=(ci, lax.rem(zi + d, n)), device_id_type=MESH)
    for j in range(bits):
        pl.semaphore_signal(barrier, inc=1, device_id=(ctx_partner(j)[0], zi), device_id_type=MESH)

    own_heads = bias_ref.shape[1]
    place = jnp.where(
        lax.broadcasted_iota(jnp.int32, (own_heads, heads), 0) + zi * own_heads
        == lax.broadcasted_iota(jnp.int32, (own_heads, heads), 1), 1.0, 0.0
    ).astype(BF16)
    for load in loads[:4]:
        load.wait()
    raw = jnp.concatenate(
        [bias_ref[...], decay_ref[...], skip_ref[...], jnp.zeros((5, own_heads), F32)], axis=0
    )
    placed = jnp.zeros((8, heads), F32)
    for part in split_terms(raw, 3):
        placed = placed + jnp.dot(part, place, preferred_element_type=F32)
    param_ref[...] = placed
    pl.semaphore_wait(barrier, n - 1 + bits)

    def remote(src, dst, sems, index, device):
        return pltpu.make_async_remote_copy(
            src_ref=src, dst_ref=dst, send_sem=sems.at[(0, *index)], recv_sem=sems.at[(1, *index)],
            device_id=device, device_id_type=MESH,
        )

    def peer(d):
        return (ci, lax.rem(zi + d, n))

    param_copies = [
        remote(param_ref, param_in.at[d], param_sems, (d,), peer(d)) for d in range(1, n)
    ]
    for copy in param_copies:
        copy.start()

    offset = lax.rem(zi * length, BLOCK)
    starts = starts_ref[...].astype(F32)
    mine = lax.broadcasted_iota(jnp.int32, starts.shape, 1) == zi * length // BLOCK
    start = jnp.sum(jnp.where(mine, starts, 0.0), axis=1, keepdims=True) - offset.astype(F32)
    start = jnp.where((start < 0.0) | (start >= length), float(length), start)
    row = lax.broadcasted_iota(jnp.int32, (length, length), 0).astype(F32)
    col = lax.broadcasted_iota(jnp.int32, (length, length), 1).astype(F32)
    lower = jnp.where(row >= col, 1.0, 0.0)
    same = jnp.where(row >= start, 1.0, 0.0) == jnp.where(col >= start, 1.0, 0.0)
    allowed = jnp.where(same, lower, 0.0)
    for load in loads[4:7]:
        load.wait()
    for g in range(groups):
        part = slice(g * STATE, (g + 1) * STATE)
        scores = lax.dot_general(
            c_ref[:, part], b_ref[:, part], (((1,), (1,)), ((), ())), preferred_element_type=F32
        )
        scores_ref[g] = jnp.where(allowed > 0.0, scores, 0.0).astype(BF16)

    for copy in param_copies:
        copy.wait()
    params = param_ref[...]
    for d in range(1, n):
        params = params + param_in[d]

    logits = logit_ref[...].astype(F32) + params[0:1]
    step = jnp.maximum(logits, 0.0) + jnp.log1p(jnp.exp(-jnp.abs(logits)))
    rate = -jnp.exp(params[1:2]) * step
    lower = lower.astype(BF16)
    cum = jnp.zeros((length, heads), F32)
    for part in split_terms(rate, 3)[::-1]:
        cum = cum + jnp.dot(lower, part, preferred_element_type=F32)
    last = cum[length - 1 : length]
    middle = cum[length // 2 - 1 : length // 2]
    position = lax.broadcasted_iota(jnp.int32, (length, heads), 0).astype(F32)
    begins = start < length
    carried = jnp.where(begins, 0.0, jnp.exp(last))

    decay_out[...] = jnp.broadcast_to(carried, decay_out.shape)
    decay_copies = [
        remote(decay_out, decay_in.at[d], decay_sems, (d,), peer(d)) for d in range(1, n)
    ]
    for copy in decay_copies:
        copy.start()
    keep = position >= jnp.where(begins, start, 0.0)
    tail = jnp.where(keep, jnp.exp(last - cum), 0.0) * step
    tail_ref[...] = jnp.concatenate(split_terms(tail, 2), axis=1)
    up_ref[...] = jnp.concatenate(split_terms(jnp.exp(cum - middle), 2), axis=1)
    down_ref[...] = jnp.concatenate(split_terms(jnp.exp(middle - cum) * step, 2), axis=1)
    loads[7].wait()
    for copy in decay_copies:
        copy.wait()
    before = jnp.ones((8, heads), F32)
    after = jnp.ones((8, heads), F32)
    for d in range(1, n):
        got = decay_in[d]
        before = before * jnp.where(zi >= d, got, 1.0)
        after = after * jnp.where(zi >= d, 1.0, got)
    own = jnp.broadcast_to(carried, (8, heads))
    total = before * own * after
    ahead = jnp.ones((8, heads), F32)
    after_parts = jnp.concatenate(split_terms(after, 2), axis=1)

    def step_copy(j, k):
        return remote(step_send.at[j, k], step_recv.at[j, k], step_sems, (j, k), (ctx_partner(j)[0], zi))

    def fore_copy(k):
        return remote(fore_send.at[k], fore_recv.at[k], fore_sems, (k,), (ci, lax.rem(zi + 1, n)))

    def back_copy(k):
        return remote(back_send.at[k], back_recv.at[k], back_sems, (k,), (ci, lax.rem(zi + n - 1, n)))

    def store_copy(k):
        channels = pl.ds(pl.multiple_of(k * CHUNK, CHUNK), CHUNK)
        return pltpu.make_async_copy(mixed_ref.at[k], mixed_hbm.at[:, channels], mixed_sems.at[k])

    def line(k, slot):
        return wide_ref[k, slot : slot + 1, :]

    is_last_upper = ctx_partner(bits - 1)[1] == 1
    is_last_lower = ctx_partner(bits - 1)[1] == 0

    def write(k, _):
        matrix = spread_matrix(heads, k * chunk_heads, CHUNK)
        weight = jnp.dot(tail_ref[...], matrix, preferred_element_type=F32)
        scale = jnp.dot(after_parts, matrix, preferred_element_type=F32)[0:1]
        channels = pl.ds(pl.multiple_of(k * CHUNK, CHUNK), CHUNK)
        scaled = (x_ref[:, channels].astype(F32) * weight).astype(BF16)
        keys = b_ref[:, pl.ds(pl.multiple_of((k // per_group) * STATE, STATE), STATE)]
        written = lax.dot_general(keys, scaled, (((0,), (0,)), ((), ())), preferred_element_type=F32)
        own_ref[k] = written
        value = written * scale
        sum_ref[k] = value
        step_send[0, k] = value.astype(BF16)
        step_copy(0, k).start()
        return 0

    middle_factor = jnp.broadcast_to(jnp.exp(middle), (8, heads))
    coefs = [middle_factor, jnp.broadcast_to(params[2:3], (8, heads)), own, before]
    for j in range(bits):
        partner, upper = ctx_partner(j)
        hop_out[j] = total
        copy = remote(hop_out.at[j], hop_in.at[j], hop_sems, (j,), (partner, zi))
        copy.start()
        lax.fori_loop(j * EARLY, (j + 1) * EARLY, write, 0)
        copy.wait()
        got = hop_in[j]
        is_upper = upper == 1
        coefs.append(jnp.where(is_upper, 1.0, got))
        coefs.append(jnp.where(is_upper, total, 1.0))
        coefs.append(jnp.where(is_upper, ahead, 0.0))
        ahead = jnp.where(is_upper, ahead * got, ahead)
        total = total * got
    slots = wide_ref.shape[1]
    pad = [jnp.zeros((1, heads), F32)] * (slots - len(coefs))
    table = jnp.concatenate([c[0:1] for c in coefs] + pad, axis=0)
    table = jnp.concatenate(split_terms(table, 2), axis=1)

    fore_at = (bits - 1 + zi) * SKEW
    back_at = (bits - 1 + n - 1 - zi) * SKEW
    done_at = jnp.maximum(fore_at, back_at)

    def iteration(t, _):
        kw = t + bits * EARLY

        @pl.when(kw < count)
        def _():
            write(kw, 0)

        for j in range(bits):
            k = t - j * SKEW

            @pl.when((k >= 0) & (k < count))
            def _(j=j, k=k):
                if j == 0:
                    matrix = spread_matrix(heads, k * chunk_heads, CHUNK)
                    wide_ref[k] = jnp.dot(table, matrix, preferred_element_type=F32)
                    before_ref[k] = jnp.zeros_like(before_ref[k])

                def receive():
                    step_copy(j, k).wait_recv()
                    got = step_recv[j, k].astype(F32)
                    before_ref[k] += line(k, 6 + 3 * j) * got
                    return got

                if j == bits - 1:
                    @pl.when(is_last_upper)
                    def _():
                        receive()

                else:
                    got = receive()
                    value = sum_ref[k] * line(k, 4 + 3 * j) + line(k, 5 + 3 * j) * got
                    sum_ref[k] = value

                    def send():
                        step_send[j + 1, k] = value.astype(BF16)
                        step_copy(j + 1, k).start()

                    if j == bits - 2:
                        pl.when(is_last_lower)(send)
                    else:
                        send()

        kf = t - fore_at

        @pl.when((kf >= 0) & (kf < count))
        def _():
            @pl.when(zi > 0)
            def _():
                fore_copy(kf).wait_recv()

            @pl.when(zi == 0)
            def _():
                fore_recv[kf] = jnp.zeros_like(fore_recv[kf])

            @pl.when(zi < n - 1)
            def _():
                arrived = fore_recv[kf].astype(F32) + line(kf, 3) * before_ref[kf]
                fore_send[kf] = (line(kf, 2) * arrived + own_ref[kf]).astype(BF16)
                fore_copy(kf).start()

        kb = t - back_at

        @pl.when((kb >= 0) & (kb < count))
        def _():
            @pl.when(zi < n - 1)
            def _():
                back_copy(kb).wait_recv()

            @pl.when(zi == n - 1)
            def _():
                back_recv[kb] = jnp.zeros_like(back_recv[kb])

            @pl.when(zi > 0)
            def _():
                back_send[kb] = (back_recv[kb].astype(F32) + before_ref[kb]).astype(BF16)
                back_copy(kb).start()

        kd = t - done_at

        @pl.when((kd >= 0) & (kd < count))
        def _():
            incoming = before_ref[kd] + back_recv[kd].astype(F32)
            frozen = (fore_recv[kd].astype(F32) + line(kd, 3) * incoming).astype(BF16)
            matrix = spread_matrix(heads, kd * chunk_heads, CHUNK)
            up = jnp.dot(up_ref[...], matrix, preferred_element_type=F32)
            down = jnp.dot(down_ref[...], matrix, preferred_element_type=F32)
            x = x_ref[:, pl.ds(pl.multiple_of(kd * CHUNK, CHUNK), CHUNK)].astype(F32)
            group = kd // per_group
            inside = jnp.dot(scores_ref[group], (x * down).astype(BF16), preferred_element_type=F32)
            queries = c_ref[:, pl.ds(pl.multiple_of(group * STATE, STATE), STATE)]
            outside = jnp.dot(queries, frozen, preferred_element_type=F32)
            place_in = lax.broadcasted_iota(jnp.int32, outside.shape, 0).astype(F32)
            outside = jnp.where(place_in < start, outside * line(kd, 0), 0.0)
            mixed_ref[kd] = (up * (inside + outside) + line(kd, 1) * x).astype(BF16)
            store_copy(kd).start()

        return 0

    lax.fori_loop(0, count + (bits - 1 + n - 1) * SKEW, iteration, 0)

    def drain(k, _):
        for j in range(bits - 1):
            step_copy(j, k).wait_send()

        @pl.when(is_last_lower)
        def _():
            step_copy(bits - 1, k).wait_send()

        @pl.when(zi < n - 1)
        def _():
            fore_copy(k).wait_send()

        @pl.when(zi > 0)
        def _():
            back_copy(k).wait_send()

        store_copy(k).wait()
        return 0

    lax.fori_loop(0, count, drain, 0)


def norm_kernel(mixed_ref, gate_ref, gain_ref, out_ref, gated_ref):
    rows, inner = mixed_ref.shape
    width = 1024
    power = jnp.zeros((rows, 1), F32)
    for i in range(inner // width):
        channels = slice(i * width, (i + 1) * width)
        gate = gate_ref[:, channels].astype(F32)
        gated = mixed_ref[:, channels].astype(F32) * (gate / (1.0 + jnp.exp(-gate)))
        gated_ref[:, channels] = gated
        power = power + jnp.sum(gated * gated, axis=1, keepdims=True)
    factor = lax.rsqrt(power / inner + 1e-05)
    for i in range(inner // width):
        channels = slice(i * width, (i + 1) * width)
        out_ref[:, channels] = (gated_ref[:, channels] * factor * gain_ref[:, channels]).astype(BF16)


def local(
    n, m,
    head_inputs, gate_inputs, write_keys, read_queries, step_logits,
    step_bias, decay_log, skip_scale, norm_gain, document_starts,
):
    length, inner = head_inputs.shape
    heads = step_logits.shape[1]
    groups = write_keys.shape[1] // STATE
    assert length <= BLOCK and BLOCK % length == 0 and m & (m - 1) == 0 and m > 1
    bits = m.bit_length() - 1
    count = inner // CHUNK

    slots = 24
    assert bits * EARLY <= count and 4 + 3 * bits <= slots
    hbm = pl.BlockSpec(memory_space=pltpu.HBM)
    anywhere = pl.BlockSpec(memory_space=pl.ANY)
    piece = (count, STATE, CHUNK)
    dma = pltpu.SemaphoreType.DMA
    mixed = pl.pallas_call(
        functools.partial(exchange_kernel, n, m, groups),
        out_shape=jax.ShapeDtypeStruct((length, inner), BF16),
        in_specs=[hbm] * 8,
        out_specs=anywhere,
        scratch_shapes=[
            pltpu.VMEM((length, inner), BF16),
            pltpu.VMEM(write_keys.shape, BF16),
            pltpu.VMEM(read_queries.shape, BF16),
            pltpu.VMEM(step_logits.shape, BF16),
            pltpu.VMEM((1, step_bias.shape[0]), F32),
            pltpu.VMEM((1, step_bias.shape[0]), F32),
            pltpu.VMEM((1, step_bias.shape[0]), F32),
            pltpu.VMEM((1, document_starts.shape[0]), jnp.int32),
            pltpu.VMEM((groups, length, length), BF16),
            pltpu.VMEM((count, length, CHUNK), BF16),
            pltpu.VMEM((8, heads), F32),
            pltpu.VMEM((length, 2 * heads), BF16),
            pltpu.VMEM((length, 2 * heads), BF16),
            pltpu.VMEM((length, 2 * heads), BF16),
            pltpu.VMEM((count, slots, CHUNK), F32),
            pltpu.VMEM(piece, F32),
            pltpu.VMEM(piece, F32),
            pltpu.VMEM(piece, F32),
            pltpu.VMEM((bits, *piece), BF16),
            pltpu.VMEM((bits, *piece), BF16),
            pltpu.VMEM(piece, BF16),
            pltpu.VMEM(piece, BF16),
            pltpu.VMEM(piece, BF16),
            pltpu.VMEM(piece, BF16),
            pltpu.VMEM((n, 8, heads), F32),
            pltpu.VMEM((8, heads), F32),
            pltpu.VMEM((n, 8, heads), F32),
            pltpu.VMEM((bits, 8, heads), F32),
            pltpu.VMEM((bits, 8, heads), F32),
            dma((2, n)),
            dma((2, n)),
            dma((2, bits)),
            dma((2, bits, count)),
            dma((2, count)),
            dma((2, count)),
            dma((8,)),
            dma((count,)),
        ],
        compiler_params=pltpu.CompilerParams(
            collective_id=0, has_side_effects=True, vmem_limit_bytes=56 * 2**20
        ),
        name="exchange",
    )(
        head_inputs, write_keys, read_queries, step_logits,
        step_bias[None], decay_log[None], skip_scale[None], document_starts[None],
    )

    tile = min(length, ROWS)
    tokens = pl.BlockSpec((tile, inner), lambda i: (i, 0))
    return pl.pallas_call(
        norm_kernel,
        grid=(length // tile,),
        out_shape=jax.ShapeDtypeStruct((length, inner), BF16),
        in_specs=[tokens, tokens, pl.BlockSpec((1, inner), lambda i: (0, 0))],
        out_specs=tokens,
        scratch_shapes=[pltpu.VMEM((tile, inner), F32)],
        compiler_params=pltpu.CompilerParams(vmem_limit_bytes=20 * 2**20),
        name="norm",
    )(mixed, gate_inputs, norm_gain[None])


def solution(mesh):
    tokens = P(("ctx", "head"), None)
    return jax.shard_map(
        functools.partial(local, mesh.shape["head"], mesh.shape["ctx"]),
        mesh=mesh,
        in_specs=(tokens,) * 5 + (P("head"), P("head"), P("head"), P(), P("ctx")),
        out_specs=tokens,
        check_vma=False,
    )
```
